768 devices in a mesh: dp: 96 (over z, y), ep: 8 (over x, core).
Axes of the slice: x: 4, y: 8, z: 12, core: 2. Of those that a mesh axis runs over, the one named last changes fastest.
Arguments:
- grad: float32 [2, 1536, 3584], P(None, 'dp', 'ep'), may hold values from -40 to 40
- momentum: float32 [2, 1536, 3584], P(None, 'dp', 'ep'), may hold values from -6 to 6
- lengths: int32 [2, 96], replicated, may hold values from 1 to 16, 1024 in all within a row
Outputs:
- new_momentum: float32 [2, 1536, 3584], P(None, 'dp', 'ep')
- update: float32 [2, 1536, 3584], P(None, 'dp', 'ep')
The draws below stay inside these ranges and needn't reach their ends.
Inputs may be any that keep to these rules, and one draw needn't show every extreme that they name: lengths[j, d] counts the rows of matrix j held by dp index d, in order of d, in the first slots of its block of 16 slots; each row of lengths sums to 1024 and reaches 16.
All inputs are finite; a program needn't handle non-finite values.
Results may differ from the reference program's by a relative error of at most 0.009.
Values may be sent and summed in bfloat16 or wider, within the bound.
No kernel may reach another device: no remote copies, remote signals or barrier semaphores. Data moves between devices by JAX's collectives and lax.ppermute only.
A program may use at most 32 MiB of HBM per device.

```python
import math
import jax
import jax.numpy as jnp
import numpy as np
from jax import lax

H = 1024
D = 3584
MATS = 2
RMAX = 16
SLOTS = 1536
N_DP = 96


def draw_grad(key, part):
    keys = jax.random.split(key, 3)
    shape = (MATS, SLOTS, D)
    row_scale = jnp.exp(jax.random.uniform(keys[1], (MATS, SLOTS, 1), jnp.float32) * math.log(10.0))
    col_scale = jnp.exp(jax.random.uniform(keys[2], (MATS, 1, D), jnp.float32) * math.log(10.0))
    base = jax.random.truncated_normal(keys[0], -4.0, 4.0, shape, jnp.float32)
    values = base * row_scale * col_scale / 10.0
    return values.astype(jnp.float32)


def levels(own_key, extent, pieces, low, top_value):
    def one(dim, shards_of):
        steps = jax.random.uniform(jax.random.fold_in(jax.random.fold_in(own_key, 6), dim), (shards_of,), jnp.float32, low / len(pieces), top_value / len(pieces))
        return jnp.repeat(jnp.exp(steps), extent[dim] // shards_of).reshape((-1,) + (1,) * (len(extent) - dim - 1))

    factor_of = one(*pieces[0])
    for cut in pieces[1:]:
        factor_of = factor_of * one(*cut)
    return factor_of


def length_profile(count, total, most, slope):
    weights = [(1 << 20) // math.isqrt(grade ** slope) + 1 for grade in range(2, count + 1)]
    rest, holding = total - most - (count - 1), [1] * (count - 1)
    while rest > 0:
        free = [i for i in range(count - 1) if holding[i] < most]
        whole, budget = sum([weights[i] for i in free]), rest
        for i in free:
            addition = min(most - holding[i], max(1, budget * weights[i] // whole), rest)
            holding[i] = holding[i] + addition
            rest = rest - addition
    return np.array([most] + holding)


def ragged_sizes(own_key, count, total, bound, slope):
    if count == 2:
        one = jax.random.randint(own_key, (), max(1, total - bound), min(bound, total - 1) + 1)
        return jnp.stack([one, total - one])
    tallies = jnp.asarray(length_profile(count, total, bound, slope), jnp.int32)
    couples = (count - 1) // 2
    source_of, sink = tallies[1:1 + 2 * couples:2], tallies[2:2 + 2 * couples:2]
    room = jnp.minimum(source_of - 1, bound - sink)
    moved = jax.random.randint(jax.random.fold_in(own_key, 1), (couples,), 0, 1 << 20) % (room + 1)
    tallies = tallies.at[1:1 + 2 * couples:2].set(source_of - moved).at[2:2 + 2 * couples:2].set(sink + moved)
    return tallies[jax.random.permutation(jax.random.fold_in(own_key, 2), count)]


def centred(own_key, dims, scale, most, cuts=(), held_as=jnp.bfloat16):
    values = jax.random.normal(own_key, dims, jnp.float32) * scale
    if len(cuts) > 0:
        values = levels(own_key, dims, cuts, -0.22, 0.18) * values
    return jnp.clip(values, min=-most, max=most).astype(held_as)


def setup_inputs(seed: int = 0) -> dict:
    arg_keys = jax.random.split(jax.random.key(seed), 4)
    return {
        "grad": draw_grad(jax.random.fold_in(arg_keys[3], 71), 0),
        "momentum": centred(arg_keys[1], (MATS, SLOTS, D), 1.0, 6.0, ((1, 96), (2, 8)), jnp.float32),
        "lengths": jax.vmap(lambda own: ragged_sizes(own, N_DP, H, RMAX, 2))(jax.random.split(arg_keys[2], MATS)).reshape((MATS, N_DP)).astype(jnp.int32),
    }


MOMENTUM_COEF = 0.95
EPSILON = 1e-06
FIRST_LIN = 3.0
FIRST_CUBE = -2.5
SECOND_LIN = 1.5
SECOND_CUBE = -0.5

def newton_polar(scaled_gram, factor, matrix):
    product = jnp.dot(scaled_gram, matrix, preferred_element_type=jnp.float32)
    first_iter = (factor * (FIRST_LIN * matrix.astype(jnp.float32) + FIRST_CUBE * product)).astype(jnp.bfloat16)
    product = jnp.dot(scaled_gram, first_iter, preferred_element_type=jnp.float32)
    applied = (FIRST_LIN * first_iter.astype(jnp.float32) + FIRST_CUBE * product).astype(jnp.bfloat16)
    second = jnp.dot(scaled_gram, applied, preferred_element_type=jnp.float32).astype(jnp.bfloat16)
    third = FIRST_LIN * second.astype(jnp.float32) + FIRST_CUBE * jnp.dot(scaled_gram, second, preferred_element_type=jnp.float32)
    return (SECOND_LIN * first_iter.astype(jnp.float32) + SECOND_CUBE * third).astype(jnp.bfloat16)

def reference(grad, momentum, lengths):
    new_momentum = MOMENTUM_COEF * momentum + grad
    rounded = (grad + MOMENTUM_COEF * new_momentum).astype(jnp.bfloat16)
    offsets = jnp.cumsum(lengths, axis=1) - lengths
    slot_ids = jnp.arange(SLOTS, dtype=jnp.int32)
    source = slot_ids // RMAX
    within = slot_ids % RMAX
    scale_out = math.sqrt(max(H, D))
    results = []
    for matrix_id in range(MATS):
        length_at = jnp.take(lengths[matrix_id], source)
        offset_at = jnp.take(offsets[matrix_id], source)
        is_valid = within < length_at
        target = jnp.where(is_valid, offset_at + within, H).astype(jnp.int32)
        matrix = jnp.zeros((H, D), jnp.bfloat16).at[target].set(rounded[matrix_id], mode='drop')
        gram = jnp.dot(matrix, matrix.T, preferred_element_type=jnp.float32)
        scale_sq = lax.rsqrt(jnp.sum(gram * gram) + EPSILON)
        scaled_gram = (scale_sq * gram).astype(jnp.bfloat16)
        ortho = newton_polar(scaled_gram, jnp.sqrt(scale_sq), matrix)
        picked = jnp.take(ortho, jnp.where(is_valid, target, 0).astype(jnp.int32), axis=0)
        results.append(jnp.where(is_valid[:, None], picked.astype(jnp.float32) * scale_out, jnp.float32(0.0)))
    return (new_momentum, jnp.stack(results))
```

```python
import math

import jax
import jax.numpy as jnp
from jax import lax
from jax.sharding import Mesh
from jax.sharding import PartitionSpec as P

H = 1024
D = 3584

MOMENTUM_COEF = 0.95
EPSILON = 1e-06
FIRST_LIN = 3.0
FIRST_CUBE = -2.5
SECOND_LIN = 1.5
SECOND_CUBE = -0.5

NZ, NY, NX, NC = 12, 8, 4, 2


def spread(block, axis, size):
    return lax.all_to_all(
        jnp.broadcast_to(block[None], (size,) + block.shape), axis, 0, 0
    )


def swap(block):
    return lax.ppermute(block, "c", [(0, 1), (1, 0)])


def sum_columns(partial):
    return jnp.sum(spread(partial, "x", NX).astype(jnp.float32), axis=0)


def rows_dot_t(rows, matrix):
    return lax.dot_general(
        rows, matrix, (((1,), (1,)), ((), ())), preferred_element_type=jnp.float32
    ).astype(jnp.bfloat16)


def rows_dot(rows, matrix):
    return jnp.dot(rows.astype(jnp.bfloat16), matrix, preferred_element_type=jnp.float32)


def body(grad, momentum, lengths):
    f32, bf16 = jnp.float32, jnp.bfloat16
    new_momentum = MOMENTUM_COEF * momentum + grad
    rounded = (grad + MOMENTUM_COEF * new_momentum).astype(bf16)
    dp = lax.axis_index("z") * NY + lax.axis_index("y")
    core = lax.axis_index("c")
    own_lengths = lax.dynamic_index_in_dim(lengths, dp, 1, keepdims=False)
    slots = lax.broadcasted_iota(jnp.int32, rounded.shape, 1)
    rounded = jnp.where(slots < own_lengths[:, None, None], rounded, jnp.zeros_like(rounded))
    first_core = core == 0
    mine = jnp.where(first_core, rounded[0], rounded[1])
    theirs = jnp.where(first_core, rounded[1], rounded[0])
    rows = jnp.concatenate([mine, swap(theirs)], axis=1)
    columns = rows.shape[1]
    matrix = spread(rows, "z", NZ).reshape(-1, columns)
    matrix = lax.all_gather(matrix, "y", axis=0, tiled=True)

    gram = sum_columns(rows_dot_t(rows, matrix))
    total_sq = jnp.broadcast_to(jnp.sum(gram * gram), (8, 128))
    total_sq = jnp.sum(spread(total_sq, "z", NZ), axis=0)
    total_sq = jnp.sum(spread(total_sq, "y", NY), axis=0)[0, 0]
    scale_sq = lax.rsqrt(total_sq + EPSILON)
    factor = jnp.sqrt(scale_sq)

    first = (
        factor * (FIRST_LIN * rows.astype(f32) + FIRST_CUBE * rows_dot(scale_sq * gram, matrix))
    ).astype(bf16)
    product = rows_dot(scale_sq * sum_columns(rows_dot_t(first, matrix)), matrix)
    applied = (FIRST_LIN * first.astype(f32) + FIRST_CUBE * product).astype(bf16)
    second = rows_dot(scale_sq * sum_columns(rows_dot_t(applied, matrix)), matrix).astype(bf16)
    product = rows_dot(scale_sq * sum_columns(rows_dot_t(second, matrix)), matrix)
    third = FIRST_LIN * second.astype(f32) + FIRST_CUBE * product
    ortho = (SECOND_LIN * first.astype(f32) + SECOND_CUBE * third).astype(bf16)

    half = columns // 2
    other = swap(ortho[:, half:])
    own = ortho[:, :half]
    update = jnp.stack([jnp.where(first_core, own, other), jnp.where(first_core, other, own)])
    return (new_momentum, update.astype(f32) * math.sqrt(max(H, D)))


def solution(mesh):
    grid = Mesh(mesh.devices.reshape(NZ, NY, NX, NC), ("z", "y", "x", "c"))
    spec = P(None, ("z", "y"), ("x", "c"))
    return jax.shard_map(
        body,
        mesh=grid,
        in_specs=(spec, spec, P()),
        out_specs=(spec, spec),
        check_vma=False,
    )
```

```python
import math

import jax
import jax.numpy as jnp
from jax import lax
from jax.sharding import Mesh
from jax.sharding import PartitionSpec as P

H = 1024
D = 3584

MOMENTUM_COEF = 0.95
EPSILON = 1e-06
FIRST_LIN = 3.0
FIRST_CUBE = -2.5
SECOND_LIN = 1.5
SECOND_CUBE = -0.5

NZ, NY, NX, NC = 12, 8, 4, 2


def spread(block, axis, size):
    return lax.all_to_all(
        jnp.broadcast_to(block[None], (size,) + block.shape), axis, 0, 0
    )


def swap(block):
    return lax.ppermute(block, "c", [(0, 1), (1, 0)])


def sum_columns(partial):
    return jnp.sum(spread(partial, "x", NX).astype(jnp.float32), axis=0)


def rows_dot_t(rows, matrix):
    return lax.dot_general(
        rows, matrix, (((1,), (1,)), ((), ())), preferred_element_type=jnp.float32
    ).astype(jnp.bfloat16)


def rows_dot(rows, matrix):
    return jnp.dot(rows.astype(jnp.bfloat16), matrix, preferred_element_type=jnp.float32)


def body(grad, momentum, lengths):
    f32, bf16 = jnp.float32, jnp.bfloat16
    new_momentum = MOMENTUM_COEF * momentum + grad
    rounded = (grad + MOMENTUM_COEF * new_momentum).astype(bf16)
    dp = lax.axis_index("z") * NY + lax.axis_index("y")
    core = lax.axis_index("c")
    own_lengths = lax.dynamic_index_in_dim(lengths, dp, 1, keepdims=False)
    slots = lax.broadcasted_iota(jnp.int32, rounded.shape, 1)
    rounded = jnp.where(slots < own_lengths[:, None, None], rounded, jnp.zeros_like(rounded))
    first_core = core == 0
    mine = jnp.where(first_core, rounded[0], rounded[1])
    theirs = jnp.where(first_core, rounded[1], rounded[0])
    rows = jnp.concatenate([mine, swap(theirs)], axis=1)
    columns = rows.shape[1]
    same_y = spread(rows, "z", NZ).reshape(-1, columns)
    matrix = lax.all_gather(same_y, "y", axis=0, tiled=True)

    rows_later, same_y = lax.optimization_barrier((rows, same_y))
    same_z = spread(rows_later, "y", NY).reshape(-1, columns)
    block = sum_columns(rows_dot_t(same_z, same_y))
    total_sq = jnp.broadcast_to(jnp.sum(block * block), (8, 128))
    total_sq = jnp.sum(spread(total_sq, "z", NZ), axis=0)[0, 0]
    block = block.reshape(NY, -1, block.shape[1])
    held = block.shape[1]
    block = jnp.concatenate(
        [block, jnp.broadcast_to(total_sq, (NY, 8, block.shape[2]))], axis=1
    )
    block = lax.all_to_all(block, "y", 0, 0)
    gram = jnp.concatenate([block[y, :held] for y in range(NY)], axis=1)
    total_sq = jnp.sum(block[:, held:], axis=0)[0, 0]
    scale_sq = lax.rsqrt(total_sq + EPSILON)
    factor = jnp.sqrt(scale_sq)

    first = (
        factor * (FIRST_LIN * rows.astype(f32) + FIRST_CUBE * rows_dot(scale_sq * gram, matrix))
    ).astype(bf16)
    product = rows_dot(scale_sq * sum_columns(rows_dot_t(first, matrix)), matrix)
    applied = (FIRST_LIN * first.astype(f32) + FIRST_CUBE * product).astype(bf16)
    second = rows_dot(scale_sq * sum_columns(rows_dot_t(applied, matrix)), matrix).astype(bf16)
    product = rows_dot(scale_sq * sum_columns(rows_dot_t(second, matrix)), matrix)
    third = FIRST_LIN * second.astype(f32) + FIRST_CUBE * product
    ortho = (SECOND_LIN * first.astype(f32) + SECOND_CUBE * third).astype(bf16)

    half = columns // 2
    other = swap(ortho[:, half:])
    own = ortho[:, :half]
    update = jnp.stack([jnp.where(first_core, own, other), jnp.where(first_core, other, own)])
    return (new_momentum, update.astype(f32) * math.sqrt(max(H, D)))


def solution(mesh):
    grid = Mesh(mesh.devices.reshape(NZ, NY, NX, NC), ("z", "y", "x", "c"))
    spec = P(None, ("z", "y"), ("x", "c"))
    return jax.shard_map(
        body,
        mesh=grid,
        in_specs=(spec, spec, P()),
        out_specs=(spec, spec),
        check_vma=False,
    )
```

```python
import math

import jax
import jax.numpy as jnp
from jax import lax
from jax.sharding import Mesh
from jax.sharding import PartitionSpec as P

H = 1024
D = 3584

MOMENTUM_COEF = 0.95
EPSILON = 1e-06
FIRST_LIN = 3.0
FIRST_CUBE = -2.5
SECOND_LIN = 1.5
SECOND_CUBE = -0.5

NZ, NY, NX, NC = 12, 8, 4, 2


def spread(block, axis, size):
    return lax.all_to_all(
        jnp.broadcast_to(block[None], (size,) + block.shape), axis, 0, 0
    )


def swap(block):
    return lax.ppermute(block, "c", [(0, 1), (1, 0)])


def sum_columns(partial):
    return jnp.sum(spread(partial, "x", NX).astype(jnp.float32), axis=0)


def rows_dot_t(rows, matrix):
    return lax.dot_general(
        rows, matrix, (((1,), (1,)), ((), ())), preferred_element_type=jnp.float32
    ).astype(jnp.bfloat16)


def rows_dot(rows, matrix):
    return jnp.dot(rows.astype(jnp.bfloat16), matrix, preferred_element_type=jnp.float32)


def body(grad, momentum, lengths):
    f32, bf16 = jnp.float32, jnp.bfloat16
    new_momentum = MOMENTUM_COEF * momentum + grad
    rounded = (grad + MOMENTUM_COEF * new_momentum).astype(bf16)
    dp = lax.axis_index("z") * NY + lax.axis_index("y")
    core = lax.axis_index("c")
    own_lengths = lax.dynamic_index_in_dim(lengths, dp, 1, keepdims=False)
    slots = lax.broadcasted_iota(jnp.int32, rounded.shape, 1)
    rounded = jnp.where(slots < own_lengths[:, None, None], rounded, jnp.zeros_like(rounded))
    first_core = core == 0
    mine = jnp.where(first_core, rounded[0], rounded[1])
    theirs = jnp.where(first_core, rounded[1], rounded[0])
    rows = jnp.concatenate([mine, swap(theirs)], axis=1)
    columns = rows.shape[1]
    same_z = spread(rows, "y", NY).reshape(-1, columns)
    rows_later, same_z = lax.optimization_barrier((rows, same_z))
    same_y = spread(rows_later, "z", NZ).reshape(-1, columns)
    matrix = lax.all_gather(same_y, "y", axis=0, tiled=True)

    block = sum_columns(rows_dot_t(same_z, same_y))
    total_sq = jnp.broadcast_to(jnp.sum(block * block), (8, 128))
    total_sq = jnp.sum(spread(total_sq, "z", NZ), axis=0)[0, 0]
    block = block.reshape(NY, -1, block.shape[1])
    held = block.shape[1]
    block = jnp.concatenate(
        [block, jnp.broadcast_to(total_sq, (NY, 8, block.shape[2]))], axis=1
    )
    block = lax.all_to_all(block, "y", 0, 0)
    gram = jnp.concatenate([block[y, :held] for y in range(NY)], axis=1)
    total_sq = jnp.sum(block[:, held:], axis=0)[0, 0]
    scale_sq = lax.rsqrt(total_sq + EPSILON)
    factor = jnp.sqrt(scale_sq)

    first = (
        factor * (FIRST_LIN * rows.astype(f32) + FIRST_CUBE * rows_dot(scale_sq * gram, matrix))
    ).astype(bf16)
    product = rows_dot(scale_sq * sum_columns(rows_dot_t(first, matrix)), matrix)
    applied = (FIRST_LIN * first.astype(f32) + FIRST_CUBE * product).astype(bf16)
    second = rows_dot(scale_sq * sum_columns(rows_dot_t(applied, matrix)), matrix).astype(bf16)
    product = rows_dot(scale_sq * sum_columns(rows_dot_t(second, matrix)), matrix)
    third = FIRST_LIN * second.astype(f32) + FIRST_CUBE * product
    ortho = (SECOND_LIN * first.astype(f32) + SECOND_CUBE * third).astype(bf16)

    half = columns // 2
    other = swap(ortho[:, half:])
    own = ortho[:, :half]
    update = jnp.stack([jnp.where(first_core, own, other), jnp.where(first_core, other, own)])
    return (new_momentum, update.astype(f32) * math.sqrt(max(H, D)))


def solution(mesh):
    grid = Mesh(mesh.devices.reshape(NZ, NY, NX, NC), ("z", "y", "x", "c"))
    spec = P(None, ("z", "y"), ("x", "c"))
    return jax.shard_map(
        body,
        mesh=grid,
        in_specs=(spec, spec, P()),
        out_specs=(spec, spec),
        check_vma=False,
    )
```

```python
import math

import jax
import jax.numpy as jnp
from jax import lax
from jax.sharding import Mesh
from jax.sharding import PartitionSpec as P

H = 1024
D = 3584

MOMENTUM_COEF = 0.95
EPSILON = 1e-06
FIRST_LIN = 3.0
FIRST_CUBE = -2.5
SECOND_LIN = 1.5
SECOND_CUBE = -0.5

NZ, NY, NX, NC = 12, 8, 4, 2
PACKED = 256


def three_parts(value):
    parts = []
    for _ in range(3):
        part = lax.reduce_precision(value, 8, 7)
        parts.append(part)
        value = value - part
    return parts


def spread(block, axis, size):
    return lax.all_to_all(
        jnp.broadcast_to(block[None], (size,) + block.shape), axis, 0, 0
    )


def swap(block):
    return lax.ppermute(block, "c", [(0, 1), (1, 0)])


def sum_columns(partial):
    return jnp.sum(spread(partial, "x", NX).astype(jnp.float32), axis=0)


def rows_dot_t(rows, matrix):
    return lax.dot_general(
        rows, matrix, (((1,), (1,)), ((), ())), preferred_element_type=jnp.float32
    ).astype(jnp.bfloat16)


def rows_dot(rows, matrix):
    return jnp.dot(rows.astype(jnp.bfloat16), matrix, preferred_element_type=jnp.float32)


def body(grad, momentum, lengths):
    f32, bf16 = jnp.float32, jnp.bfloat16
    new_momentum = MOMENTUM_COEF * momentum + grad
    rounded = (grad + MOMENTUM_COEF * new_momentum).astype(bf16)
    dp = lax.axis_index("z") * NY + lax.axis_index("y")
    core = lax.axis_index("c")
    own_lengths = lax.dynamic_index_in_dim(lengths, dp, 1, keepdims=False)
    slots = lax.broadcasted_iota(jnp.int32, rounded.shape, 1)
    rounded = jnp.where(slots < own_lengths[:, None, None], rounded, jnp.zeros_like(rounded))
    first_core = core == 0
    mine = jnp.where(first_core, rounded[0], rounded[1])
    theirs = jnp.where(first_core, rounded[1], rounded[0])
    rows = jnp.concatenate([mine, swap(theirs)], axis=1)
    columns = rows.shape[1]
    same_y = spread(rows, "z", NZ).reshape(-1, columns)
    matrix = lax.all_gather(same_y, "y", axis=0, tiled=True)

    rows_later, same_y = lax.optimization_barrier((rows, same_y))
    same_z = spread(rows_later, "y", NY).reshape(-1, columns)
    block = sum_columns(rows_dot_t(same_z, same_y))
    total_sq = jnp.broadcast_to(jnp.sum(block * block, keepdims=True), (1, 128))
    total_sq = jnp.sum(spread(total_sq, "z", NZ), axis=0)
    block = block.astype(bf16).reshape(NY, -1, block.shape[1])
    held = block.shape[2]
    shape = block.shape[:2] + (PACKED - held,)
    lane = lax.broadcasted_iota(jnp.int32, shape, 2)
    packed = jnp.zeros(shape, f32)
    for k, part in enumerate(three_parts(total_sq[:, : shape[2]])):
        packed = jnp.where(lane == k, part[None], packed)
    block = jnp.concatenate([block, packed.astype(bf16)], axis=2)
    block = lax.all_to_all(block, "y", 0, 0)
    gram = jnp.concatenate([block[y, :, :held] for y in range(NY)], axis=1)
    total_sq = jnp.sum(block[:, :1, held:].astype(f32))
    scale_sq = lax.rsqrt(total_sq + EPSILON)
    factor = jnp.sqrt(scale_sq)

    first = (
        factor * (FIRST_LIN * rows.astype(f32) + FIRST_CUBE * (scale_sq * rows_dot(gram, matrix)))
    ).astype(bf16)
    product = rows_dot(scale_sq * sum_columns(rows_dot_t(first, matrix)), matrix)
    applied = (FIRST_LIN * first.astype(f32) + FIRST_CUBE * product).astype(bf16)
    second = rows_dot(scale_sq * sum_columns(rows_dot_t(applied, matrix)), matrix).astype(bf16)
    product = rows_dot(scale_sq * sum_columns(rows_dot_t(second, matrix)), matrix)
    third = FIRST_LIN * second.astype(f32) + FIRST_CUBE * product
    ortho = (SECOND_LIN * first.astype(f32) + SECOND_CUBE * third).astype(bf16)

    half = columns // 2
    other = swap(ortho[:, half:])
    own = ortho[:, :half]
    update = jnp.stack([jnp.where(first_core, own, other), jnp.where(first_core, other, own)])
    return (new_momentum, update.astype(f32) * math.sqrt(max(H, D)))


def solution(mesh):
    grid = Mesh(mesh.devices.reshape(NZ, NY, NX, NC), ("z", "y", "x", "c"))
    spec = P(None, ("z", "y"), ("x", "c"))
    return jax.shard_map(
        body,
        mesh=grid,
        in_specs=(spec, spec, P()),
        out_specs=(spec, spec),
        check_vma=False,
    )
```

```python
import math

import jax
import jax.numpy as jnp
from jax import lax
from jax.sharding import Mesh
from jax.sharding import PartitionSpec as P

H = 1024
D = 3584

MOMENTUM_COEF = 0.95
EPSILON = 1e-06
FIRST_LIN = 3.0
FIRST_CUBE = -2.5
SECOND_LIN = 1.5
SECOND_CUBE = -0.5

NZ, NY, NX, NC = 12, 8, 4, 2
PACKED = 256
TINY = 1e-30
SMALL = 2.0**-34


def polynomial():
    def times(p, q):
        out = [0.0] * (len(p) + len(q) - 1)
        for i, a in enumerate(p):
            for j, b in enumerate(q):
                out[i + j] += a * b
        return out

    step = [FIRST_LIN, FIRST_CUBE]
    inner = [0.0] + [SECOND_CUBE * v for v in times(step, step)]
    inner[0] = SECOND_LIN
    return times(step, inner)


COEFS = polynomial()


def expansion(coefs, at):
    out = []
    for order in range(len(coefs)):
        value = 0.0
        for power in range(len(coefs) - 1, order - 1, -1):
            value = value * at + math.comb(power, order) * coefs[power]
        out.append(value)
    return out


def along_z(value, shift):
    return lax.ppermute(value, "z", [(z, (z + shift) % NZ) for z in range(NZ)])


def three_parts(value):
    parts = []
    for _ in range(3):
        part = lax.reduce_precision(value, 8, 7)
        parts.append(part)
        value = value - part
    return parts


def spread(block, axis, size):
    return lax.all_to_all(
        jnp.broadcast_to(block[None], (size,) + block.shape), axis, 0, 0
    )


def swap(block):
    return lax.ppermute(block, "c", [(0, 1), (1, 0)])


def sum_columns(partial):
    return jnp.sum(spread(partial, "x", NX).astype(jnp.float32), axis=0)


def rows_dot_t(rows, matrix):
    return lax.dot_general(
        rows, matrix, (((1,), (1,)), ((), ())), preferred_element_type=jnp.float32
    ).astype(jnp.bfloat16)


def rows_dot(rows, matrix):
    return jnp.dot(rows.astype(jnp.bfloat16), matrix, preferred_element_type=jnp.float32)


def body(grad, momentum, lengths):
    f32, bf16 = jnp.float32, jnp.bfloat16
    new_momentum = MOMENTUM_COEF * momentum + grad
    rounded = (grad + MOMENTUM_COEF * new_momentum).astype(bf16)
    dp = lax.axis_index("z") * NY + lax.axis_index("y")
    core = lax.axis_index("c")
    own_lengths = lax.dynamic_index_in_dim(lengths, dp, 1, keepdims=False)
    slots = lax.broadcasted_iota(jnp.int32, rounded.shape, 1)
    rounded = jnp.where(slots < own_lengths[:, None, None], rounded, jnp.zeros_like(rounded))
    first_core = core == 0
    mine = jnp.where(first_core, rounded[0], rounded[1])
    theirs = jnp.where(first_core, rounded[1], rounded[0])
    rows = jnp.concatenate([mine, swap(theirs)], axis=1)
    columns = rows.shape[1]
    same_y = spread(rows, "z", NZ).reshape(-1, columns)
    matrix = lax.all_gather(same_y, "y", axis=0, tiled=True)

    rows_later, same_y = lax.optimization_barrier((rows, same_y))
    same_z = spread(rows_later, "y", NY).reshape(-1, columns)
    block = sum_columns(rows_dot_t(same_z, same_y))
    parts = three_parts(jnp.sum(block * block))
    block = block.astype(bf16).reshape(NY, -1, block.shape[1])
    held = block.shape[2]
    lane = lax.broadcasted_iota(jnp.int32, block.shape[:2] + (PACKED - held,), 2)
    packed = jnp.zeros(lane.shape, f32)
    for k, part in enumerate(parts):
        packed = jnp.where(lane == k, part, packed)
    block = jnp.concatenate([block, packed.astype(bf16)], axis=2)
    block = lax.all_to_all(block, "y", 0, 0)
    gram = jnp.concatenate([block[y, :, :held] for y in range(NY)], axis=1)
    total_sq = jnp.broadcast_to(jnp.sum(block[:, :1, held:].astype(f32)), (8, 128))

    row = lax.broadcasted_iota(jnp.int32, gram.shape, 0)
    column = lax.broadcasted_iota(jnp.int32, gram.shape, 1)
    place = lax.axis_index("y") * held + lax.axis_index("z") * gram.shape[0]
    wide = gram.astype(f32)
    diagonal = jnp.sum(jnp.where(column == place + row, wide, 0.0), axis=1, keepdims=True)
    shift = jnp.sum(wide * wide, axis=1, keepdims=True) / jnp.maximum(diagonal, TINY)
    weights = gram * SMALL
    before = rows.astype(f32) * SMALL
    terms = []
    moving = [along_z(total_sq, step) for step in (1, 2)]
    for phase in range(3):
        product = rows_dot(weights, matrix)
        terms.append(product)
        before = product - shift * before
        weights = rows_dot_t(before.astype(bf16), matrix)
        if phase > 0:
            total_sq, moving, weights = lax.optimization_barrier((total_sq, moving, weights))
            total_sq = total_sq + sum(moving)
        if phase == 1:
            moving = [along_z(total_sq, step) for step in (3, 6, 9)]
        weights = sum_columns(weights)
    terms.append(rows_dot(weights, matrix))
    scale_sq = lax.rsqrt(total_sq[:1, :1] + EPSILON)
    factor = jnp.sqrt(scale_sq)
    taylor = expansion(COEFS[1:], scale_sq * shift)
    tail = taylor[3] * terms[3]
    for k in (2, 1, 0):
        tail = scale_sq * tail + taylor[k] * terms[k]
    tail = (scale_sq / SMALL) * tail
    ortho = (factor * (COEFS[0] * rows.astype(f32) + tail)).astype(bf16)

    half = columns // 2
    other = swap(ortho[:, half:])
    own = ortho[:, :half]
    update = jnp.stack([jnp.where(first_core, own, other), jnp.where(first_core, other, own)])
    return (new_momentum, update.astype(f32) * math.sqrt(max(H, D)))


def solution(mesh):
    grid = Mesh(mesh.devices.reshape(NZ, NY, NX, NC), ("z", "y", "x", "c"))
    spec = P(None, ("z", "y"), ("x", "c"))
    return jax.shard_map(
        body,
        mesh=grid,
        in_specs=(spec, spec, P()),
        out_specs=(spec, spec),
        check_vma=False,
    )
```

```python
import math

import jax
import jax.numpy as jnp
from jax import lax
from jax.sharding import Mesh
from jax.sharding import PartitionSpec as P

H = 1024
D = 3584

MOMENTUM_COEF = 0.95
EPSILON = 1e-06
FIRST_LIN = 3.0
FIRST_CUBE = -2.5
SECOND_LIN = 1.5
SECOND_CUBE = -0.5

NZ, NY, NX, NC = 12, 8, 4, 2
PACKED = 256


def three_parts(value):
    parts = []
    for _ in range(3):
        part = lax.reduce_precision(value, 8, 7)
        parts.append(part)
        value = value - part
    return parts


def spread(block, axis, size):
    return lax.all_to_all(
        jnp.broadcast_to(block[None], (size,) + block.shape), axis, 0, 0
    )


def swap(block):
    return lax.ppermute(block, "c", [(0, 1), (1, 0)])


def sum_columns(partial):
    return jnp.sum(spread(partial, "x", NX).astype(jnp.float32), axis=0)


def rows_dot_t(rows, matrix):
    return lax.dot_general(
        rows, matrix, (((1,), (1,)), ((), ())), preferred_element_type=jnp.float32
    ).astype(jnp.bfloat16)


def rows_dot(rows, matrix):
    return jnp.dot(rows.astype(jnp.bfloat16), matrix, preferred_element_type=jnp.float32)


def body(grad, momentum, lengths):
    f32, bf16 = jnp.float32, jnp.bfloat16
    new_momentum = MOMENTUM_COEF * momentum + grad
    rounded = (grad + MOMENTUM_COEF * new_momentum).astype(bf16)
    dp = lax.axis_index("z") * NY + lax.axis_index("y")
    core = lax.axis_index("c")
    own_lengths = lax.dynamic_index_in_dim(lengths, dp, 1, keepdims=False)
    slots = lax.broadcasted_iota(jnp.int32, rounded.shape, 1)
    rounded = jnp.where(slots < own_lengths[:, None, None], rounded, jnp.zeros_like(rounded))
    first_core = core == 0
    mine = jnp.where(first_core, rounded[0], rounded[1])
    theirs = jnp.where(first_core, rounded[1], rounded[0])
    rows = jnp.concatenate([mine, swap(theirs)], axis=1)
    columns = rows.shape[1]
    same_y = spread(rows, "z", NZ).reshape(-1, columns)
    matrix = lax.all_gather(same_y, "y", axis=0, tiled=True)

    rows_later, same_y = lax.optimization_barrier((rows, same_y))
    same_z = spread(rows_later, "y", NY).reshape(-1, columns)
    block = sum_columns(rows_dot_t(same_z, same_y))
    squares = jnp.sum(block * block, axis=0, keepdims=True)
    block = block.astype(bf16).reshape(NY, -1, block.shape[1])
    held = block.shape[2]
    spare = PACKED - held
    squares = sum(squares[:, k : k + spare] for k in range(0, held, spare))
    line = lax.broadcasted_iota(jnp.int32, (block.shape[1], spare), 0)
    packed = jnp.zeros(line.shape, f32)
    for k, part in enumerate(three_parts(squares)):
        packed = jnp.where(line == k, part, packed)
    packed = jnp.broadcast_to(packed.astype(bf16), (NY,) + packed.shape)
    block = lax.all_to_all(jnp.concatenate([block, packed], axis=2), "y", 0, 0)
    gram = jnp.concatenate([block[y, :, :held] for y in range(NY)], axis=1)
    squares = jnp.sum(block[:, :, held:].astype(f32), axis=(0, 1))[None]
    squares = spread(jnp.concatenate([squares, jnp.zeros_like(squares)], axis=1), "z", NZ)
    product = rows_dot(gram, matrix)
    product, squares = lax.optimization_barrier((product, squares))
    total_sq = jnp.sum(squares)
    scale_sq = lax.rsqrt(total_sq + EPSILON)
    factor = jnp.sqrt(scale_sq)
    first = (factor * (FIRST_LIN * rows.astype(f32) + (FIRST_CUBE * scale_sq) * product)).astype(bf16)
    product = rows_dot(scale_sq * sum_columns(rows_dot_t(first, matrix)), matrix)
    applied = (FIRST_LIN * first.astype(f32) + FIRST_CUBE * product).astype(bf16)
    second = rows_dot(scale_sq * sum_columns(rows_dot_t(applied, matrix)), matrix).astype(bf16)
    product = rows_dot(scale_sq * sum_columns(rows_dot_t(second, matrix)), matrix)
    third = FIRST_LIN * second.astype(f32) + FIRST_CUBE * product
    ortho = (SECOND_LIN * first.astype(f32) + SECOND_CUBE * third).astype(bf16)

    half = columns // 2
    other = swap(ortho[:, half:])
    own = ortho[:, :half]
    update = jnp.stack([jnp.where(first_core, own, other), jnp.where(first_core, other, own)])
    return (new_momentum, update.astype(f32) * math.sqrt(max(H, D)))


def solution(mesh):
    grid = Mesh(mesh.devices.reshape(NZ, NY, NX, NC), ("z", "y", "x", "c"))
    spec = P(None, ("z", "y"), ("x", "c"))
    return jax.shard_map(
        body,
        mesh=grid,
        in_specs=(spec, spec, P()),
        out_specs=(spec, spec),
        check_vma=False,
    )
```

```python
import math

import jax
import jax.numpy as jnp
from jax import lax
from jax.sharding import Mesh
from jax.sharding import PartitionSpec as P

H = 1024
D = 3584

MOMENTUM_COEF = 0.95
EPSILON = 1e-06
FIRST_LIN = 3.0
FIRST_CUBE = -2.5
SECOND_LIN = 1.5
SECOND_CUBE = -0.5

NZ, NY, NX, NC = 12, 8, 4, 2
PACKED = 256


def three_parts(value):
    parts = []
    for _ in range(3):
        part = lax.reduce_precision(value, 8, 7)
        parts.append(part)
        value = value - part
    return parts


def spread(block, axis, size):
    return lax.all_to_all(
        jnp.broadcast_to(block[None], (size,) + block.shape), axis, 0, 0
    )


def swap(block):
    return lax.ppermute(block, "c", [(0, 1), (1, 0)])


def sum_columns(partial):
    return jnp.sum(spread(partial, "x", NX).astype(jnp.float32), axis=0)


def rows_dot_t(rows, matrix):
    return lax.dot_general(
        rows, matrix, (((1,), (1,)), ((), ())), preferred_element_type=jnp.float32
    ).astype(jnp.bfloat16)


def rows_dot(rows, matrix):
    return jnp.dot(rows.astype(jnp.bfloat16), matrix, preferred_element_type=jnp.float32)


def body(grad, momentum, lengths):
    f32, bf16 = jnp.float32, jnp.bfloat16
    new_momentum = MOMENTUM_COEF * momentum + grad
    rounded = (grad + MOMENTUM_COEF * new_momentum).astype(bf16)
    dp = lax.axis_index("z") * NY + lax.axis_index("y")
    core = lax.axis_index("c")
    first_core = core == 0
    mine = jnp.where(first_core, rounded[0], rounded[1])
    theirs = jnp.where(first_core, rounded[1], rounded[0])
    rows = jnp.concatenate([mine, swap(theirs)], axis=1)
    columns = rows.shape[1]
    own_length = lax.dynamic_slice(lengths, (core, dp), (1, 1))
    slots = lax.broadcasted_iota(jnp.int32, rows.shape, 0)
    rows = jnp.where(slots < own_length, rows, jnp.zeros_like(rows))
    same_y = spread(rows, "z", NZ).reshape(-1, columns)
    matrix = lax.all_gather(same_y, "y", axis=0, tiled=True)

    rows_later, same_y = lax.optimization_barrier((rows, same_y))
    same_z = spread(rows_later, "y", NY).reshape(-1, columns)
    block = sum_columns(rows_dot_t(same_z, same_y))
    squares = jnp.sum(block * block, axis=0, keepdims=True)
    block = block.astype(bf16).reshape(NY, -1, block.shape[1])
    held = block.shape[2]
    spare = PACKED - held
    squares = sum(squares[:, k : k + spare] for k in range(0, held, spare))
    parts = three_parts(squares)
    blank = jnp.broadcast_to(0.0 * parts[-1], (block.shape[1] - len(parts), spare))
    packed = jnp.concatenate(parts + [blank], axis=0)
    packed = jnp.broadcast_to(packed.astype(bf16), (NY,) + packed.shape)
    block = lax.all_to_all(jnp.concatenate([block, packed], axis=2), "y", 0, 0)
    gram = jnp.concatenate([block[y, :, :held] for y in range(NY)], axis=1)
    squares = jnp.sum(block[:, :, held:].astype(f32), axis=(0, 1))[None]
    squares = spread(jnp.concatenate([squares, jnp.zeros_like(squares)], axis=1), "z", NZ)
    product = rows_dot(gram, matrix)
    product, squares = lax.optimization_barrier((product, squares))
    total_sq = jnp.sum(squares)
    scale_sq = lax.rsqrt(total_sq + EPSILON)
    factor = jnp.sqrt(scale_sq)
    first = (factor * (FIRST_LIN * rows.astype(f32) + (FIRST_CUBE * scale_sq) * product)).astype(bf16)
    product = rows_dot(scale_sq * sum_columns(rows_dot_t(first, matrix)), matrix)
    applied = (FIRST_LIN * first.astype(f32) + FIRST_CUBE * product).astype(bf16)
    second = rows_dot(scale_sq * sum_columns(rows_dot_t(applied, matrix)), matrix).astype(bf16)
    product = rows_dot(scale_sq * sum_columns(rows_dot_t(second, matrix)), matrix)
    third = FIRST_LIN * second.astype(f32) + FIRST_CUBE * product
    ortho = (SECOND_LIN * first.astype(f32) + SECOND_CUBE * third).astype(bf16)

    half = columns // 2
    other = swap(ortho[:, half:])
    own = ortho[:, :half]
    update = jnp.stack([jnp.where(first_core, own, other), jnp.where(first_core, other, own)])
    return (new_momentum, update.astype(f32) * math.sqrt(max(H, D)))


def solution(mesh):
    grid = Mesh(mesh.devices.reshape(NZ, NY, NX, NC), ("z", "y", "x", "c"))
    spec = P(None, ("z", "y"), ("x", "c"))
    return jax.shard_map(
        body,
        mesh=grid,
        in_specs=(spec, spec, P()),
        out_specs=(spec, spec),
        check_vma=False,
    )
```

```python
import math

import jax
import jax.numpy as jnp
from jax import lax
from jax.sharding import Mesh
from jax.sharding import PartitionSpec as P

H = 1024
D = 3584

MOMENTUM_COEF = 0.95
EPSILON = 1e-06
FIRST_LIN = 3.0
FIRST_CUBE = -2.5
SECOND_LIN = 1.5
SECOND_CUBE = -0.5

NZ, NY, NX, NC = 12, 8, 4, 2
PACKED = 256


def three_parts(value):
    parts = []
    for _ in range(3):
        part = lax.reduce_precision(value, 8, 7)
        parts.append(part)
        value = value - part
    return parts


def spread(block, axis, size):
    return lax.all_to_all(
        jnp.broadcast_to(block[None], (size,) + block.shape), axis, 0, 0
    )


def swap(block):
    return lax.ppermute(block, "c", [(0, 1), (1, 0)])


def sum_columns(partial):
    return jnp.sum(spread(partial, "x", NX).astype(jnp.float32), axis=0)


def rows_dot_t(rows, matrix):
    return lax.dot_general(
        rows, matrix, (((1,), (1,)), ((), ())), preferred_element_type=jnp.float32
    ).astype(jnp.bfloat16)


def rows_dot(rows, matrix):
    return jnp.dot(rows.astype(jnp.bfloat16), matrix, preferred_element_type=jnp.float32)


def body(grad, momentum, lengths):
    f32, bf16 = jnp.float32, jnp.bfloat16
    new_momentum = MOMENTUM_COEF * momentum + grad
    rounded = (grad + MOMENTUM_COEF * new_momentum).astype(bf16)
    dp = lax.axis_index("z") * NY + lax.axis_index("y")
    core = lax.axis_index("c")
    first_core = core == 0
    mine = jnp.where(first_core, rounded[0], rounded[1])
    theirs = jnp.where(first_core, rounded[1], rounded[0])
    rows = jnp.concatenate([mine, swap(theirs)], axis=1)
    columns = rows.shape[1]
    own_length = lax.dynamic_slice(lengths, (core, dp), (1, 1))
    slots = lax.broadcasted_iota(jnp.int32, rows.shape, 0)
    rows = jnp.where(slots < own_length, rows, jnp.zeros_like(rows))
    same_z = spread(rows, "y", NY).reshape(-1, columns)
    matrix = lax.all_gather(same_z, "z", axis=0, tiled=True)

    rows_later, same_z = lax.optimization_barrier((rows, same_z))
    same_y = spread(rows_later, "z", NZ).reshape(-1, columns)
    block = sum_columns(rows_dot_t(same_y, same_z))
    squares = jnp.sum(block * block, axis=0, keepdims=True)
    block = block.astype(bf16).reshape(NZ, -1, block.shape[1])
    held = block.shape[2]
    spare = PACKED - held
    parts = three_parts(squares)
    blank = jnp.broadcast_to(0.0 * parts[-1], (block.shape[1] - len(parts), spare))
    packed = jnp.concatenate(parts + [blank], axis=0)
    packed = jnp.broadcast_to(packed.astype(bf16), (NZ,) + packed.shape)
    block = lax.all_to_all(jnp.concatenate([block, packed], axis=2), "z", 0, 0)
    gram = jnp.concatenate([block[z, :, :held] for z in range(NZ)], axis=1)
    squares = jnp.sum(block[:, :, held:].astype(f32), axis=(0, 1))[None]
    squares = spread(squares, "y", NY)
    product = rows_dot(gram, matrix)
    product, squares = lax.optimization_barrier((product, squares))
    total_sq = jnp.sum(squares)
    scale_sq = lax.rsqrt(total_sq + EPSILON)
    factor = jnp.sqrt(scale_sq)
    first = (factor * (FIRST_LIN * rows.astype(f32) + (FIRST_CUBE * scale_sq) * product)).astype(bf16)
    product = rows_dot(scale_sq * sum_columns(rows_dot_t(first, matrix)), matrix)
    applied = (FIRST_LIN * first.astype(f32) + FIRST_CUBE * product).astype(bf16)
    second = rows_dot(scale_sq * sum_columns(rows_dot_t(applied, matrix)), matrix).astype(bf16)
    product = rows_dot(scale_sq * sum_columns(rows_dot_t(second, matrix)), matrix)
    third = FIRST_LIN * second.astype(f32) + FIRST_CUBE * product
    ortho = (SECOND_LIN * first.astype(f32) + SECOND_CUBE * third).astype(bf16)

    half = columns // 2
    other = swap(ortho[:, half:])
    own = ortho[:, :half]
    update = jnp.stack([jnp.where(first_core, own, other), jnp.where(first_core, other, own)])
    return (new_momentum, update.astype(f32) * math.sqrt(max(H, D)))


def solution(mesh):
    grid = Mesh(mesh.devices.reshape(NZ, NY, NX, NC), ("z", "y", "x", "c"))
    spec = P(None, ("z", "y"), ("x", "c"))
    return jax.shard_map(
        body,
        mesh=grid,
        in_specs=(spec, spec, P()),
        out_specs=(spec, spec),
        check_vma=False,
    )
```

```python
import math

import jax
import jax.numpy as jnp
from jax import lax
from jax.sharding import Mesh
from jax.sharding import PartitionSpec as P

H = 1024
D = 3584

MOMENTUM_COEF = 0.95
EPSILON = 1e-06
FIRST_LIN = 3.0
FIRST_CUBE = -2.5
SECOND_LIN = 1.5
SECOND_CUBE = -0.5

NZ, NY, NX, NC = 12, 8, 4, 2
PACKED = 256


def three_parts(value):
    parts = []
    for _ in range(3):
        part = lax.reduce_precision(value, 8, 7)
        parts.append(part)
        value = value - part
    return parts


def spread(block, axis, size):
    return lax.all_to_all(
        jnp.broadcast_to(block[None], (size,) + block.shape), axis, 0, 0
    )


def swap(block):
    return lax.ppermute(block, "c", [(0, 1), (1, 0)])


def sum_columns(partial):
    return jnp.sum(spread(partial, "x", NX).astype(jnp.float32), axis=0)


def rows_dot_t(rows, matrix):
    return lax.dot_general(
        rows, matrix, (((1,), (1,)), ((), ())), preferred_element_type=jnp.float32
    ).astype(jnp.bfloat16)


def rows_dot(rows, matrix):
    return jnp.dot(rows.astype(jnp.bfloat16), matrix, preferred_element_type=jnp.float32)


def body(grad, momentum, lengths):
    f32, bf16 = jnp.float32, jnp.bfloat16
    new_momentum = MOMENTUM_COEF * momentum + grad
    rounded = (grad + MOMENTUM_COEF * new_momentum).astype(bf16)
    dp = lax.axis_index("z") * NY + lax.axis_index("y")
    core = lax.axis_index("c")
    first_core = core == 0
    mine = jnp.where(first_core, rounded[0], rounded[1])
    theirs = jnp.where(first_core, rounded[1], rounded[0])
    rows = jnp.concatenate([mine, swap(theirs)], axis=1)
    columns = rows.shape[1]
    own_length = lax.dynamic_slice(lengths, (core, dp), (1, 1))
    slots = lax.broadcasted_iota(jnp.int32, rows.shape, 0)
    rows = jnp.where(slots < own_length, rows, jnp.zeros_like(rows))
    same_z = spread(rows, "y", NY).reshape(-1, columns)
    matrix = lax.all_gather(same_z, "z", axis=0, tiled=True)

    rows_later, same_z = lax.optimization_barrier((rows, same_z))
    same_y = spread(rows_later, "z", NZ).reshape(-1, columns)
    block = sum_columns(rows_dot_t(same_y, same_z))
    squares = jnp.sum(block * block, axis=0, keepdims=True)
    block = block.astype(bf16).reshape(NZ, -1, block.shape[1])
    held = block.shape[2]
    spare = PACKED - held
    parts = three_parts(squares)
    blank = jnp.broadcast_to(0.0 * parts[-1], (block.shape[1] - len(parts), spare))
    packed = jnp.concatenate(parts + [blank], axis=0)
    packed = jnp.broadcast_to(packed.astype(bf16), (NZ,) + packed.shape)
    block = lax.all_to_all(jnp.concatenate([block, packed], axis=2), "z", 0, 0)
    gram = lax.optimization_barrier(
        jnp.swapaxes(block[:, :, :held], 0, 1).reshape(block.shape[1], -1)
    )
    squares = jnp.sum(block[:, :, held:].astype(f32), axis=(0, 1))[None]
    squares = spread(squares, "y", NY)
    product = rows_dot(gram, matrix)
    product, squares = lax.optimization_barrier((product, squares))
    total_sq = jnp.sum(squares)
    scale_sq = lax.rsqrt(total_sq + EPSILON)
    factor = jnp.sqrt(scale_sq)
    first = (factor * (FIRST_LIN * rows.astype(f32) + (FIRST_CUBE * scale_sq) * product)).astype(bf16)
    product = rows_dot(scale_sq * sum_columns(rows_dot_t(first, matrix)), matrix)
    applied = (FIRST_LIN * first.astype(f32) + FIRST_CUBE * product).astype(bf16)
    second = rows_dot(scale_sq * sum_columns(rows_dot_t(applied, matrix)), matrix).astype(bf16)
    product = rows_dot(scale_sq * sum_columns(rows_dot_t(second, matrix)), matrix)
    third = FIRST_LIN * second.astype(f32) + FIRST_CUBE * product
    ortho = (SECOND_LIN * first.astype(f32) + SECOND_CUBE * third).astype(bf16)

    half = columns // 2
    other = swap(ortho[:, half:])
    own = ortho[:, :half]
    update = jnp.stack([jnp.where(first_core, own, other), jnp.where(first_core, other, own)])
    return (new_momentum, update.astype(f32) * math.sqrt(max(H, D)))


def solution(mesh):
    grid = Mesh(mesh.devices.reshape(NZ, NY, NX, NC), ("z", "y", "x", "c"))
    spec = P(None, ("z", "y"), ("x", "c"))
    return jax.shard_map(
        body,
        mesh=grid,
        in_specs=(spec, spec, P()),
        out_specs=(spec, spec),
        check_vma=False,
    )
```

```python
import math

import jax
import jax.numpy as jnp
from jax import lax
from jax.sharding import Mesh
from jax.sharding import PartitionSpec as P

H = 1024
D = 3584

MOMENTUM_COEF = 0.95
EPSILON = 1e-06
FIRST_LIN = 3.0
FIRST_CUBE = -2.5
SECOND_LIN = 1.5
SECOND_CUBE = -0.5

NZ, NY, NX, NC = 12, 8, 4, 2
PACKED = 256


def three_parts(value):
    parts = []
    for _ in range(3):
        part = lax.reduce_precision(value, 8, 7)
        parts.append(part)
        value = value - part
    return parts


def spread(block, axis, size):
    return lax.all_to_all(
        jnp.broadcast_to(block[None], (size,) + block.shape), axis, 0, 0
    )


def swap(block):
    return lax.ppermute(block, "c", [(0, 1), (1, 0)])


def sum_columns(partial):
    return jnp.sum(spread(partial, "x", NX).astype(jnp.float32), axis=0)


def rows_dot_t(rows, matrix):
    return lax.dot_general(
        rows, matrix, (((1,), (1,)), ((), ())), preferred_element_type=jnp.float32
    ).astype(jnp.bfloat16)


def rows_dot(rows, matrix):
    return jnp.dot(rows.astype(jnp.bfloat16), matrix, preferred_element_type=jnp.float32)


def body(grad, momentum, lengths):
    f32, bf16 = jnp.float32, jnp.bfloat16
    rounded = (grad + MOMENTUM_COEF * (MOMENTUM_COEF * momentum + grad)).astype(bf16)
    dp = lax.axis_index("z") * NY + lax.axis_index("y")
    core = lax.axis_index("c")
    first_core = core == 0
    mine = jnp.where(first_core, rounded[0], rounded[1])
    theirs = jnp.where(first_core, rounded[1], rounded[0])
    rows = jnp.concatenate([mine, swap(theirs)], axis=1)
    columns = rows.shape[1]
    own_length = lax.dynamic_slice(lengths, (core, dp), (1, 1))
    slots = lax.broadcasted_iota(jnp.int32, rows.shape, 0)
    rows = jnp.where(slots < own_length, rows, jnp.zeros_like(rows))
    same_y = spread(rows, "z", NZ).reshape(-1, columns)
    matrix = lax.all_gather(same_y, "y", axis=0, tiled=True)

    rows_later, same_y, grad, momentum = lax.optimization_barrier((rows, same_y, grad, momentum))
    new_momentum = MOMENTUM_COEF * momentum + grad
    same_z = spread(rows_later, "y", NY).reshape(-1, columns)
    block = sum_columns(rows_dot_t(same_z, same_y))
    squares = jnp.sum(block * block, axis=0, keepdims=True)
    block = block.astype(bf16).reshape(NY, -1, block.shape[1])
    held = block.shape[2]
    spare = PACKED - held
    squares = sum(squares[:, k : k + spare] for k in range(0, held, spare))
    parts = three_parts(squares)
    blank = jnp.broadcast_to(0.0 * parts[-1], (block.shape[1] - len(parts), spare))
    packed = jnp.concatenate(parts + [blank], axis=0)
    packed = jnp.broadcast_to(packed.astype(bf16), (NY,) + packed.shape)
    block = lax.all_to_all(jnp.concatenate([block, packed], axis=2), "y", 0, 0)
    gram = jnp.concatenate([block[y, :, :held] for y in range(NY)], axis=1)
    squares = jnp.sum(block[:, :, held:].astype(f32), axis=(0, 1))[None]
    squares = spread(jnp.concatenate([squares, jnp.zeros_like(squares)], axis=1), "z", NZ)
    product = rows_dot(gram, matrix)
    product, squares = lax.optimization_barrier((product, squares))
    total_sq = jnp.sum(squares)
    scale_sq = lax.rsqrt(total_sq + EPSILON)
    factor = jnp.sqrt(scale_sq)
    first = (factor * (FIRST_LIN * rows.astype(f32) + (FIRST_CUBE * scale_sq) * product)).astype(bf16)
    product = rows_dot(scale_sq * sum_columns(rows_dot_t(first, matrix)), matrix)
    applied = (FIRST_LIN * first.astype(f32) + FIRST_CUBE * product).astype(bf16)
    second = rows_dot(scale_sq * sum_columns(rows_dot_t(applied, matrix)), matrix).astype(bf16)
    product = rows_dot(scale_sq * sum_columns(rows_dot_t(second, matrix)), matrix)
    third = FIRST_LIN * second.astype(f32) + FIRST_CUBE * product
    ortho = (SECOND_LIN * first.astype(f32) + SECOND_CUBE * third).astype(bf16)

    half = columns // 2
    other = swap(ortho[:, half:])
    own = ortho[:, :half]
    update = jnp.stack([jnp.where(first_core, own, other), jnp.where(first_core, other, own)])
    return (new_momentum, update.astype(f32) * math.sqrt(max(H, D)))


def solution(mesh):
    grid = Mesh(mesh.devices.reshape(NZ, NY, NX, NC), ("z", "y", "x", "c"))
    spec = P(None, ("z", "y"), ("x", "c"))
    return jax.shard_map(
        body,
        mesh=grid,
        in_specs=(spec, spec, P()),
        out_specs=(spec, spec),
        check_vma=False,
    )
```
